256 devices in a mesh: mp: 2 (over z_hi), dp: 8 (over y, core), tensor: 16 (over z_lo, x).
Axes of the slice: x: 4, y: 4, z: 8 (z_hi: 2, z_lo: 4; z = z_hi * 4 + z_lo), core: 2. Of those that a mesh axis runs over, the one named last changes fastest.
Arguments:
- activations: bfloat16 [2, 1024, 8192], P('mp', 'dp'), may hold values from -6 to 6
- gate_pre: bfloat16 [2, 1024, 28672], P('mp', 'dp', 'tensor'), may hold values from -6 to 6
- hidden_grad: bfloat16 [2, 1024, 28672], P('mp', 'dp', 'tensor'), may hold values from -1.2 to 1.2, as said below
- up_weights: bfloat16 [2, 8192, 28672], P('mp', 'dp', 'tensor'), may hold values from -6 to 6
Outputs:
- merged: bfloat16 [8192, 28672], P(('dp', 'mp'), 'tensor')
The draws below stay inside these ranges and needn't reach their ends.
Inputs may be any that keep to these rules, and one draw needn't show every extreme that they name: `hidden_grad`: each sequence's values share one scale, spread evenly in the logarithm between 0.005 and 0.3 over sequences.
All inputs are finite; a program needn't handle non-finite values.
Results may differ from the reference program's by a relative error of at most 0.003.
Values may be sent and summed in bfloat16 or wider, within the bound.
No kernel may reach another device: no remote copies, remote signals or barrier semaphores. Data moves between devices by JAX's collectives and lax.ppermute only.
A program may use at most 192 MiB of HBM per device.

```python
import math
import jax
import jax.numpy as jnp
from jax import lax

D = 8192
FF = 28672
LEN = 128
SEQS = 8
TOKENS = 1024
MODELS = 2
N_TENSOR = 16


def draw_activations(key, part):
    key_common = jax.random.fold_in(key, 31)
    key_own = jax.random.fold_in(key, 37)
    common = jax.random.normal(key_common, (MODELS, SEQS, 1, D), jnp.float32)
    own = jax.random.normal(key_own, (MODELS, SEQS, LEN, D), jnp.float32)
    base = 0.8 * common + 0.6 * own
    values = jnp.clip(base, -6.0, 6.0).reshape(MODELS, SEQS * LEN, D)
    return values.astype(jnp.bfloat16)


def draw_hidden_grad(key, part):
    key_scale = jax.random.fold_in(key, 11)
    key_base = jax.random.fold_in(key, 23)
    key_common = jax.random.fold_in(key, 29)
    scales = jnp.exp(jax.random.uniform(key_scale, (MODELS, SEQS, 1, 1), jnp.float32, math.log(0.005), math.log(0.3)))
    common = jax.random.normal(key_common, (MODELS, SEQS, 1, FF), jnp.float32)
    own = jax.random.normal(key_base, (MODELS, SEQS, LEN, FF), jnp.float32)
    base = 0.8 * common + 0.6 * own
    values = (scales * jnp.clip(base, -4.0, 4.0)).reshape(MODELS, SEQS * LEN, FF)
    return values.astype(jnp.bfloat16)


def levels(stream_key, extent, split, least, largest):
    def one(position, blocks):
        steps = jax.random.uniform(jax.random.fold_in(jax.random.fold_in(stream_key, 6), position), (blocks,), jnp.float32, least / len(split), largest / len(split))
        return jnp.repeat(jnp.exp(steps), extent[position] // blocks).reshape((-1,) + (1,) * (len(extent) - position - 1))

    loudness = one(*split[0])
    for cut in split[1:]:
        loudness = loudness * one(*cut)
    return loudness


def scatter_about(key, extent, deviation, most, shards=(), kind=jnp.bfloat16):
    level = levels(key, extent, shards, -0.22, 0.18) if shards else 1.0
    array = jax.random.normal(key, extent, jnp.float32) * deviation * level
    return jnp.minimum(jnp.maximum(array, -most), most).astype(kind)


def setup_inputs(seed: int = 0) -> dict:
    key_list = jax.random.split(jax.random.key(seed), 5)
    activations = draw_activations(jax.random.fold_in(key_list[4], 71), 0)
    gate_pre = scatter_about(key_list[1], (MODELS, TOKENS, FF), 1.0, 6.0, ((0, 2), (1, 8), (2, 16)))
    hidden_grad = draw_hidden_grad(jax.random.fold_in(key_list[4], 71), 0)
    up_weights = scatter_about(key_list[3], (MODELS, D, FF), 1.0, 6.0, ((0, 2), (1, 8), (2, 16)))
    return {"activations": activations, "gate_pre": gate_pre, "hidden_grad": hidden_grad, "up_weights": up_weights}


clip_ratio = 0.05
fisher_floor = 0.1

def reference(activations, gate_pre, hidden_grad, up_weights):
    single_precision = jnp.float32
    cot_low = lax.optimization_barrier((hidden_grad.astype(single_precision) * jax.nn.silu(gate_pre.astype(single_precision))).astype(jnp.bfloat16))
    cot_seq = cot_low.astype(single_precision).reshape(MODELS, SEQS, LEN, FF)
    sequence_inputs = activations.astype(single_precision).reshape(MODELS, SEQS, LEN, D)
    input_gram_matrix = jnp.einsum('msld,msnd->msln', sequence_inputs, sequence_inputs)
    gram_cot = jnp.einsum('mslf,msnf->msln', cot_seq, cot_seq)
    grad_norm = jnp.sqrt(lax.optimization_barrier(jnp.sum(input_gram_matrix * gram_cot, axis=(2, 3))))
    clip_limit = clip_ratio * (LEN * D * FF) ** 0.5
    factor = clip_limit / jnp.maximum(grad_norm, clip_limit)
    clip_sq = factor * factor
    block = FF // N_TENSOR

    def column_block(index):
        begin = (index * block).astype(jnp.int32)
        columns = lax.dynamic_slice_in_dim(cot_seq, begin, block, 3)
        weight_cols = lax.dynamic_slice_in_dim(up_weights, begin, block, 2).astype(single_precision)

        def add_seq(total, seq_index):
            grad = jnp.einsum('mld,mlf->mdf', sequence_inputs[:, seq_index], columns[:, seq_index])
            return (total + clip_sq[:, seq_index, None, None] * grad * grad, None)
        fisher, unused = lax.scan(add_seq, jnp.zeros((MODELS, D, block), single_precision), jnp.arange(SEQS, dtype=jnp.int32))
        weighted = fisher + fisher_floor
        return (lax.optimization_barrier(jnp.sum(weighted * weight_cols, axis=0)) / lax.optimization_barrier(jnp.sum(weighted, axis=0))).astype(jnp.bfloat16)
    stacked = lax.map(column_block, jnp.arange(N_TENSOR, dtype=jnp.int32))
    return jnp.transpose(stacked, (1, 0, 2)).reshape(D, FF)
```

```python
import functools
import math

import jax
import jax.numpy as jnp
from jax import lax
from jax.experimental import pallas as pl
from jax.experimental.pallas import tpu as pltpu
from jax.sharding import PartitionSpec as P


D = 8192
FF = 28672
LEN = 128
CLIP_RATIO = 0.05
FLOOR = 0.1

N_Y, N_CORE, N_Z, N_X = 4, 2, 4, 4
N_DP = N_Y * N_CORE
N_TENSOR = N_Z * N_X
N_MP = 2
MP_SWAP = [(0, 1), (1, 0)]
CORE_SWAP = [(i, i ^ 1) for i in range(N_DP)]
VMEM_LIMIT = 50 * 1024 * 1024


def exchange(value, axis):
    return lax.all_to_all(value, axis, 0, 0, tiled=True)


def y_shift(k):
    return [
        (y * N_CORE + c, (y + k) % N_Y * N_CORE + c) for y in range(N_Y) for c in range(N_CORE)
    ]


def x_shift(k):
    return [(z * N_X + x, z * N_X + (x + k) % N_X) for z in range(N_Z) for x in range(N_X)]


def prep_kernel(where, x_ref, cot_ref, own_ref, other_ref, part_ref):
    mine, col = where[0], where[1]
    inputs = x_ref[...]
    gram_act = lax.dot_general(
        inputs, inputs, (((1,), (1,)), ((), ())), preferred_element_type=jnp.float32
    )
    cot = cot_ref[...]
    gram_cot = lax.dot_general(
        cot, cot, (((1,), (1,)), ((), ())), preferred_element_type=jnp.float32
    )
    part_ref[...] = jnp.full(part_ref.shape, jnp.sum(gram_act * gram_cot), jnp.float32)
    for d in range(N_DP):
        for ref, half in ((own_ref, mine), (other_ref, 1 - mine)):
            start = pl.multiple_of(((d * N_MP + half) * N_X + col) * 128, 128)
            ref[d] = x_ref[:, pl.ds(start, 128)].T


def fisher_kernel(n_seq, where, scale, *refs):
    x_refs = refs[:N_X]
    cots = (refs[N_X : N_X + n_seq], refs[N_X + n_seq : N_X + 2 * n_seq])
    w_ref, a_ref, b_ref, lhs = refs[N_X + 2 * n_seq :]
    @pl.when(pl.program_id(0) == 0)
    def _():
        for piece in range(N_X):
            rows = pl.ds(pl.multiple_of(where[piece] * 128, 128), 128)
            for seq in range(n_seq):
                for model in range(2):
                    lhs[model, seq, rows, :] = x_refs[piece][seq, model]

    for block in range(4):
        rows = pl.ds(block * 128, 128)
        weighted = []
        for model in range(2):
            total = jnp.full((128, a_ref.shape[1]), FLOOR, jnp.float32)
            for piece in range(n_seq):
                seq = where[N_X + piece]
                grad = jnp.dot(
                    lhs[model, seq, rows, :],
                    cots[model][piece][...],
                    preferred_element_type=jnp.float32,
                )
                total = total + scale[seq * 2 + model] * (grad * grad)
            weighted.append(total)
        inverse = 1.0 / (weighted[0] + weighted[1])
        a_ref[rows, :] = weighted[0] * inverse * w_ref[rows, :].astype(jnp.float32)
        b_ref[rows, :] = weighted[1] * inverse


def merge_kernel(a_ref, b_ref, w_ref, *refs):
    out_ref = refs[-1]
    out_ref[...] = (a_ref[...] + b_ref[...] * w_ref[...].astype(jnp.float32)).astype(jnp.bfloat16)


def local(activations, gate_pre, hidden_grad, up_weights):
    single = jnp.float32
    width = gate_pre.shape[2]
    m = lax.axis_index("mp").astype(jnp.int32)
    d = lax.axis_index("dp").astype(jnp.int32)
    x = lax.rem(lax.axis_index("tensor").astype(jnp.int32), N_X)
    rows = up_weights.shape[1] // N_MP

    cot = (hidden_grad[0].astype(single) * jax.nn.silu(gate_pre[0].astype(single))).astype(
        jnp.bfloat16
    )
    cot_other = lax.ppermute(cot, "mp", MP_SWAP)

    piece_shape = jax.ShapeDtypeStruct((N_DP, 128, LEN), jnp.bfloat16)
    own_x, other_x, part = pl.pallas_call(
        prep_kernel,
        out_shape=(piece_shape, piece_shape, jax.ShapeDtypeStruct((8, 128), single)),
        grid_spec=pltpu.PrefetchScalarGridSpec(
            num_scalar_prefetch=1,
            grid=(1,),
            in_specs=[
                pl.BlockSpec((LEN, D), lambda i, w: (0, 0)),
                pl.BlockSpec((LEN, width), lambda i, w: (0, 0)),
            ],
            out_specs=[
                pl.BlockSpec((N_DP, 128, LEN), lambda i, w: (0, 0, 0)),
                pl.BlockSpec((N_DP, 128, LEN), lambda i, w: (0, 0, 0)),
                pl.BlockSpec((8, 128), lambda i, w: (0, 0)),
            ],
        ),
        compiler_params=pltpu.CompilerParams(vmem_limit_bytes=VMEM_LIMIT),
        cost_estimate=pl.CostEstimate(flops=4 * 10**8, bytes_accessed=4 * 10**6, transcendentals=0),
        name="prep",
    )(jnp.stack([m, x]), activations[0], cot)

    sent = jnp.broadcast_to(part[None, :1], (N_MP * N_TENSOR, 1, 128))
    parts = exchange(sent, ("mp", "tensor"))
    square = jnp.sum(parts.reshape(N_MP, N_TENSOR, 128), axis=1)
    square = jnp.stack([square[m], square[1 - m]])
    squares = exchange(jnp.broadcast_to(square[None], (N_DP, N_MP, 128)), "dp")
    norm = jnp.sqrt(squares[:, :, 0])
    clip_limit = CLIP_RATIO * math.sqrt(LEN * D * FF)
    factor = clip_limit / jnp.maximum(norm, clip_limit)
    scale = (factor * factor).reshape(-1)

    from_other = lax.ppermute(other_x, "mp", MP_SWAP)
    x_pieces = exchange(jnp.stack([own_x, from_other], axis=1), "dp")
    x_all = [x_pieces] + [lax.ppermute(x_pieces, "tensor", x_shift(k)) for k in (1, -1, 2)]
    x_from = [x, lax.rem(x + 3, 4), lax.rem(x + 1, 4), lax.rem(x + 2, 4)]

    n_chunk = 4
    chunk = rows // n_chunk
    w_mine = up_weights[0]
    w_other = []
    for k in range(n_chunk):
        piece = lax.dynamic_slice(w_mine, ((1 - m) * rows + k * chunk, 0), (chunk, width))
        w_other.append(lax.ppermute(piece, "mp", MP_SWAP))

    y = d // N_CORE
    c = lax.rem(d, N_CORE)
    cots, seqs = [], []
    for value in (cot, cot_other):
        pieces = [value] + [lax.ppermute(value, "dp", y_shift(k)) for k in (1, -1, 2)]
        pieces += [lax.ppermute(piece, "dp", CORE_SWAP) for piece in pieces]
        cots += pieces
    for core in (c, 1 - c):
        for shift in (0, 3, 1, 2):
            seqs.append(lax.rem(y + shift, N_Y) * N_CORE + core)

    tile = 256
    n_seq = N_DP
    where = jnp.stack(x_from + seqs).astype(jnp.int32)
    whole = pl.BlockSpec((N_DP, 2, 128, LEN), lambda i, *_: (0, 0, 0, 0))
    a, b = pl.pallas_call(
        functools.partial(fisher_kernel, n_seq),
        out_shape=(
            jax.ShapeDtypeStruct((rows, width), single),
            jax.ShapeDtypeStruct((rows, width), single),
        ),
        grid_spec=pltpu.PrefetchScalarGridSpec(
            num_scalar_prefetch=2,
            grid=(width // tile,),
            in_specs=[whole] * N_X
            + [pl.BlockSpec((LEN, tile), lambda i, *_: (0, i))] * (2 * n_seq)
            + [pl.BlockSpec((rows, tile), lambda i, w, s: (w[N_X + n_seq], i))],
            out_specs=[pl.BlockSpec((rows, tile), lambda i, *_: (0, i))] * 2,
            scratch_shapes=[pltpu.VMEM((2, n_seq, rows, LEN), jnp.bfloat16)],
        ),
        compiler_params=pltpu.CompilerParams(vmem_limit_bytes=VMEM_LIMIT),
        cost_estimate=pl.CostEstimate(flops=4 * 10**9, bytes_accessed=18 * 10**6, transcendentals=0),
        name="fisher",
    )(jnp.concatenate([where, m[None]]), scale, *x_all, *cots, up_weights[0])

    out = None
    for k in range(n_chunk):
        half = lambda i, k=k: (k, 0)
        first = lambda i: (0, 0)
        in_specs = [pl.BlockSpec((chunk, width), half)] * 2 + [pl.BlockSpec((chunk, width), first)]
        operands = [a, b, w_other[k]]
        aliases = {}
        if out is not None:
            in_specs.append(pl.BlockSpec(memory_space=pl.ANY))
            operands.append(out)
            aliases = {3: 0}
        out = pl.pallas_call(
            merge_kernel,
            out_shape=jax.ShapeDtypeStruct((rows, width), jnp.bfloat16),
            grid=(1,),
            in_specs=in_specs,
            out_specs=pl.BlockSpec((chunk, width), half),
            input_output_aliases=aliases,
            compiler_params=pltpu.CompilerParams(vmem_limit_bytes=VMEM_LIMIT),
            cost_estimate=pl.CostEstimate(
                flops=chunk * width * 2, bytes_accessed=chunk * width * 12, transcendentals=0
            ),
        )(*operands)
    return out


def solution(mesh):
    placed = (
        P("mp", "dp", None),
        P("mp", "dp", "tensor"),
        P("mp", "dp", "tensor"),
        P("mp", "dp", "tensor"),
    )

    return jax.shard_map(
        local, mesh=mesh, in_specs=placed, out_specs=P(("dp", "mp"), "tensor"), check_vma=False
    )
```

```python
import functools
import math

import jax
import jax.numpy as jnp
from jax import lax
from jax.experimental import pallas as pl
from jax.experimental.pallas import tpu as pltpu
from jax.sharding import PartitionSpec as P


D = 8192
FF = 28672
LEN = 128
CLIP_RATIO = 0.05
FLOOR = 0.1

N_Y, N_CORE, N_Z, N_X = 4, 2, 4, 4
N_DP = N_Y * N_CORE
N_MP = 2
MP_SWAP = [(0, 1), (1, 0)]
Z_SWAP = [(z * N_X + x, (z ^ 1) * N_X + x) for z in range(N_Z) for x in range(N_X)]
HALF = N_DP // 2
CORE_SWAP = [(i, i ^ 1) for i in range(N_DP)]
VMEM_LIMIT = 50 * 1024 * 1024
PREP_VMEM_LIMIT = 63 * 1024 * 1024


CHUNKS = ((384, 128), (0, 256), (288, 96), (256, 32))
Z_GROUPS = [
    [(m * N_Z + z) * N_X + x for m in range(N_MP) for z in range(N_Z)] for x in range(N_X)
]
N_Z_ALL = N_MP * N_Z
TAIL = 8


def exchange(value, axis, groups=None):
    return lax.all_to_all(value, axis, 0, 0, axis_index_groups=groups, tiled=True)


def y_shift(k):
    return [
        (y * N_CORE + c, (y + k) % N_Y * N_CORE + c) for y in range(N_Y) for c in range(N_CORE)
    ]


def x_shift(k):
    return [(z * N_X + x, z * N_X + (x + k) % N_X) for z in range(N_Z) for x in range(N_X)]


def piece_kernel(where, *refs):
    *x_refs, w_ref, out_ref, chunk_ref = refs
    for d, ref in enumerate(x_refs):
        out_ref[d] = ref[...].T
    chunk_ref[...] = w_ref[...]


def prep_kernel(where, x_hbm, gate_ref, grad_ref, own_ref, cot_ref, part_ref, x_ref, arrived):
    mine, col = where[0], where[1]
    parts = x_ref.shape[0]
    copies = [
        pltpu.make_async_copy(
            x_hbm.at[:, pl.ds(k * x_ref.shape[2], x_ref.shape[2])], x_ref.at[k], arrived.at[k]
        )
        for k in range(parts)
    ]
    for copy in copies:
        copy.start()
    gate = gate_ref[...].astype(jnp.float32)
    silu = gate / (1.0 + jnp.exp(-gate))
    cot = (grad_ref[...].astype(jnp.float32) * silu).astype(jnp.bfloat16)
    cot_ref[...] = cot
    gram_cot = lax.dot_general(
        cot, cot, (((1,), (1,)), ((), ())), preferred_element_type=jnp.float32
    )
    gram_act = jnp.zeros((LEN, LEN), jnp.float32)
    share = N_DP // parts
    for k in range(parts):
        copies[k].wait()
        inputs = x_ref[k]
        gram_act += lax.dot_general(
            inputs, inputs, (((1,), (1,)), ((), ())), preferred_element_type=jnp.float32
        )
        for d in range(share):
            start = pl.multiple_of(((d * N_MP + mine) * N_X + col) * 128, 128)
            own_ref[k * share + d] = x_ref[k, :, pl.ds(start, 128)].T
    part_ref[...] = jnp.full(part_ref.shape, jnp.sum(gram_act * gram_cot), jnp.float32)


def pack_kernel(where, own_ref, kept_ref, swapped_ref, part_ref, out_ref):
    parity = where[2]
    rows = []
    for model in range(N_MP):
        rest = jnp.sum(part_ref[pl.ds(model * N_Z, N_Z), 0, :], axis=0, keepdims=True)
        for _ in range(3):
            short = rest.astype(jnp.bfloat16).astype(jnp.float32)
            rows.append(short)
            rest = rest - short
    rows.append(jnp.zeros((TAIL - len(rows), 128), jnp.float32))
    tail = jnp.concatenate(rows, axis=0).astype(jnp.bfloat16)
    for d in range(N_DP):
        out_ref[d, 0, pl.ds(0, 128), :] = own_ref[d]
        for model in range(2):
            out_ref[d, model, pl.ds(128, TAIL), :] = tail
    for half, ref in ((parity, kept_ref), (1 - parity, swapped_ref)):
        for d in range(HALF):
            out_ref[half * HALF + d, 1, pl.ds(0, 128), :] = ref[d]


def fisher_kernel(n_seq, where, *refs):
    x_refs = refs[:N_X]
    cots = (refs[N_X : N_X + n_seq], refs[N_X + n_seq : N_X + 2 * n_seq])
    w_ref, a_ref, b_ref, lhs, scale = refs[N_X + 2 * n_seq :]
    first = where[N_X + n_seq] == 0
    limit = CLIP_RATIO * math.sqrt(LEN * D * FF)

    @pl.when(pl.program_id(0) == 0)
    def _():
        for piece in range(N_X):
            rows = pl.ds(pl.multiple_of(where[piece] * 128, 128), 128)
            for seq in range(n_seq):
                for model in range(2):
                    lhs[model, seq, rows, :] = x_refs[piece][seq, model, pl.ds(0, 128), :]
        for seq in range(n_seq):
            tails = sum(
                ref[seq, 0, pl.ds(128, TAIL), :].astype(jnp.float32) for ref in x_refs
            )
            squares = [tails[3 * k : 3 * k + 1] + tails[3 * k + 1 : 3 * k + 2] + tails[3 * k + 2 : 3 * k + 3] for k in range(2)]
            for model in range(2):
                square = jnp.where(first, squares[model], squares[1 - model])
                factor = limit / jnp.maximum(jnp.sqrt(square), limit)
                clip = factor * factor
                scale[model, seq] = jnp.broadcast_to(
                    jnp.concatenate([clip] * (scale.shape[3] // 128), axis=1), scale.shape[2:]
                )

    for block in range(4):
        rows = pl.ds(block * 128, 128)
        weighted = []
        for model in range(2):
            total = jnp.full((128, a_ref.shape[1]), FLOOR, jnp.float32)
            for piece in range(n_seq):
                seq = where[N_X + piece]
                grad = jnp.dot(
                    lhs[model, seq, rows, :],
                    cots[model][piece][...],
                    preferred_element_type=jnp.float32,
                )
                total = total + scale[model, seq, pl.ds(0, 1), :] * (grad * grad)
            weighted.append(total)
        inverse = 1.0 / (weighted[0] + weighted[1])
        a_ref[rows, :] = weighted[0] * inverse * w_ref[rows, :].astype(jnp.float32)
        b_ref[rows, :] = weighted[1] * inverse


def merge_kernel(a_ref, b_ref, w_ref, *refs):
    out_ref = refs[-1]
    out_ref[...] = (a_ref[...] + b_ref[...] * w_ref[...].astype(jnp.float32)).astype(jnp.bfloat16)


def local(activations, gate_pre, hidden_grad, up_weights):
    single = jnp.float32
    width = gate_pre.shape[2]
    m = lax.axis_index("mp").astype(jnp.int32)
    d = lax.axis_index("dp").astype(jnp.int32)
    x = lax.rem(lax.axis_index("tensor").astype(jnp.int32), N_X)
    rows = up_weights.shape[1] // N_MP

    parity = lax.rem(lax.axis_index("tensor").astype(jnp.int32) // N_X, 2)
    place = jnp.stack([m, x, parity])
    first_row, first_size = CHUNKS[0]
    first_block = first_row // first_size
    half_blocks = rows // first_size
    piece_shape = jax.ShapeDtypeStruct((N_DP, 128, LEN), jnp.bfloat16)
    half_shape = (HALF, 128, LEN)
    other_x, w_first = pl.pallas_call(
        piece_kernel,
        out_shape=(
            jax.ShapeDtypeStruct(half_shape, jnp.bfloat16),
            jax.ShapeDtypeStruct((first_size, width), jnp.bfloat16),
        ),
        grid_spec=pltpu.PrefetchScalarGridSpec(
            num_scalar_prefetch=1,
            grid=(1,),
            in_specs=[
                pl.BlockSpec(
                    (LEN, 128),
                    lambda i, w, d=d: (0, ((w[2] * HALF + d) * N_MP + 1 - w[0]) * N_X + w[1]),
                )
                for d in range(HALF)
            ]
            + [
                pl.BlockSpec(
                    (first_size, width), lambda i, w: ((1 - w[0]) * half_blocks + first_block, 0)
                )
            ],
            out_specs=[
                pl.BlockSpec(half_shape, lambda i, w: (0, 0, 0)),
                pl.BlockSpec((first_size, width), lambda i, w: (0, 0)),
            ],
        ),
        compiler_params=pltpu.CompilerParams(vmem_limit_bytes=PREP_VMEM_LIMIT),
        cost_estimate=pl.CostEstimate(flops=10**5, bytes_accessed=10**6, transcendentals=0),
        name="pieces",
    )(place, *[activations[0]] * HALF, up_weights[0])

    copies = 4
    still = lambda i, w: (0, 0)
    own_x, cot, part = pl.pallas_call(
        prep_kernel,
        out_shape=(
            piece_shape,
            jax.ShapeDtypeStruct((LEN, width), jnp.bfloat16),
            jax.ShapeDtypeStruct((N_Z_ALL, 1, 128), single),
        ),
        grid_spec=pltpu.PrefetchScalarGridSpec(
            num_scalar_prefetch=1,
            grid=(1,),
            in_specs=[
                pl.BlockSpec(memory_space=pl.ANY),
                pl.BlockSpec((LEN, width), still),
                pl.BlockSpec((LEN, width), still),
            ],
            out_specs=[
                pl.BlockSpec((N_DP, 128, LEN), lambda i, w: (0, 0, 0)),
                pl.BlockSpec((LEN, width), still),
                pl.BlockSpec((N_Z_ALL, 1, 128), lambda i, w: (0, 0, 0)),
            ],
            scratch_shapes=[
                pltpu.VMEM((copies, LEN, D // copies), jnp.bfloat16),
                pltpu.SemaphoreType.DMA((copies,)),
            ],
        ),
        compiler_params=pltpu.CompilerParams(vmem_limit_bytes=PREP_VMEM_LIMIT),
        cost_estimate=pl.CostEstimate(flops=4 * 10**8, bytes_accessed=4 * 10**6, transcendentals=0),
        name="prep",
    )(place, activations[0], gate_pre[0], hidden_grad[0])
    cot_other = lax.ppermute(cot, "mp", MP_SWAP)

    from_other = lax.ppermute(other_x, "mp", MP_SWAP)
    parts = exchange(part, ("mp", "tensor"), Z_GROUPS)
    swapped = lax.ppermute(from_other, "tensor", Z_SWAP)
    packed = pl.pallas_call(
        pack_kernel,
        out_shape=jax.ShapeDtypeStruct((N_DP, 2, 128 + TAIL, LEN), jnp.bfloat16),
        grid_spec=pltpu.PrefetchScalarGridSpec(
            num_scalar_prefetch=1,
            grid=(1,),
            in_specs=[
                pl.BlockSpec((N_DP, 128, LEN), lambda i, w: (0, 0, 0)),
                pl.BlockSpec(half_shape, lambda i, w: (0, 0, 0)),
                pl.BlockSpec(half_shape, lambda i, w: (0, 0, 0)),
                pl.BlockSpec((N_Z_ALL, 1, 128), lambda i, w: (0, 0, 0)),
            ],
            out_specs=pl.BlockSpec((N_DP, 2, 128 + TAIL, LEN), lambda i, w: (0, 0, 0, 0)),
        ),
        compiler_params=pltpu.CompilerParams(vmem_limit_bytes=VMEM_LIMIT),
        cost_estimate=pl.CostEstimate(flops=10**5, bytes_accessed=10**6, transcendentals=0),
        name="pack",
    )(place, own_x, from_other, swapped, parts)
    x_pieces = exchange(packed, "dp")
    x_all = [x_pieces] + [lax.ppermute(x_pieces, "tensor", x_shift(k)) for k in (1, -1, 2)]
    x_from = [x, lax.rem(x + 3, 4), lax.rem(x + 1, 4), lax.rem(x + 2, 4)]

    w_later, _ = lax.optimization_barrier((up_weights[0], cot))
    w_other = []
    for k, (begin, size) in enumerate(CHUNKS):
        piece = w_first
        if k:
            piece = lax.dynamic_slice(w_later, ((1 - m) * rows + begin, 0), (size, width))
        w_other.append(lax.ppermute(piece, "mp", MP_SWAP))

    y = d // N_CORE
    c = lax.rem(d, N_CORE)
    cots, seqs = [], []
    for value in (cot, cot_other):
        pieces = [value] + [lax.ppermute(value, "dp", y_shift(k)) for k in (1, -1, 2)]
        pieces += [lax.ppermute(piece, "dp", CORE_SWAP) for piece in pieces]
        cots += pieces
    for core in (c, 1 - c):
        for shift in (0, 3, 1, 2):
            seqs.append(lax.rem(y + shift, N_Y) * N_CORE + core)

    tile = 256
    n_seq = N_DP
    where = jnp.stack(x_from + seqs).astype(jnp.int32)
    whole = pl.BlockSpec((N_DP, 2, 128 + TAIL, LEN), lambda i, *_: (0, 0, 0, 0))
    a, b = pl.pallas_call(
        functools.partial(fisher_kernel, n_seq),
        out_shape=(
            jax.ShapeDtypeStruct((rows, width), single),
            jax.ShapeDtypeStruct((rows, width), single),
        ),
        grid_spec=pltpu.PrefetchScalarGridSpec(
            num_scalar_prefetch=1,
            grid=(width // tile,),
            in_specs=[whole] * N_X
            + [pl.BlockSpec((LEN, tile), lambda i, *_: (0, i))] * (2 * n_seq)
            + [pl.BlockSpec((rows, tile), lambda i, w: (w[N_X + n_seq], i))],
            out_specs=[pl.BlockSpec((rows, tile), lambda i, *_: (0, i))] * 2,
            scratch_shapes=[
                pltpu.VMEM((2, n_seq, rows, LEN), jnp.bfloat16),
                pltpu.VMEM((2, n_seq, 8, tile), single),
            ],
        ),
        compiler_params=pltpu.CompilerParams(vmem_limit_bytes=VMEM_LIMIT),
        cost_estimate=pl.CostEstimate(flops=4 * 10**9, bytes_accessed=18 * 10**6, transcendentals=0),
        name="fisher",
    )(jnp.concatenate([where, m[None]]), *x_all, *cots, up_weights[0])

    out = None
    for k, (begin, chunk) in enumerate(CHUNKS):
        half = lambda i, k=begin // chunk: (k, 0)
        first = lambda i: (0, 0)
        in_specs = [pl.BlockSpec((chunk, width), half)] * 2 + [pl.BlockSpec((chunk, width), first)]
        operands = [a, b, w_other[k]]
        aliases = {}
        if out is not None:
            in_specs.append(pl.BlockSpec(memory_space=pl.ANY))
            operands.append(out)
            aliases = {3: 0}
        out = pl.pallas_call(
            merge_kernel,
            out_shape=jax.ShapeDtypeStruct((rows, width), jnp.bfloat16),
            grid=(1,),
            in_specs=in_specs,
            out_specs=pl.BlockSpec((chunk, width), half),
            input_output_aliases=aliases,
            compiler_params=pltpu.CompilerParams(vmem_limit_bytes=VMEM_LIMIT),
            cost_estimate=pl.CostEstimate(
                flops=chunk * width * 2, bytes_accessed=chunk * width * 12, transcendentals=0
            ),
        )(*operands)
    return out


def solution(mesh):
    placed = (
        P("mp", "dp", None),
        P("mp", "dp", "tensor"),
        P("mp", "dp", "tensor"),
        P("mp", "dp", "tensor"),
    )

    return jax.shard_map(
        local, mesh=mesh, in_specs=placed, out_specs=P(("dp", "mp"), "tensor"), check_vma=False
    )
```

```python
import functools
import math

import jax
import jax.numpy as jnp
from jax import lax
from jax.experimental import pallas as pl
from jax.experimental.pallas import tpu as pltpu
from jax.sharding import PartitionSpec as P


D = 8192
FF = 28672
LEN = 128
CLIP_RATIO = 0.05
FLOOR = 0.1

N_Y, N_CORE, N_Z, N_X = 4, 2, 4, 4
N_DP = N_Y * N_CORE
N_MP = 2
MP_SWAP = [(0, 1), (1, 0)]
Z_SWAP = [(z * N_X + x, (z ^ 1) * N_X + x) for z in range(N_Z) for x in range(N_X)]
HALF = N_DP // 2
CORE_SWAP = [(i, i ^ 1) for i in range(N_DP)]
VMEM_LIMIT = 50 * 1024 * 1024
PREP_VMEM_LIMIT = 63 * 1024 * 1024


CHUNKS = ((256, 128), (0, 256), (384, 96), (480, 32))
Z_GROUPS = [
    [(m * N_Z + z) * N_X + x for m in range(N_MP) for z in range(N_Z)] for x in range(N_X)
]
N_Z_ALL = N_MP * N_Z
TAIL = 8


def exchange(value, axis, groups=None):
    return lax.all_to_all(value, axis, 0, 0, axis_index_groups=groups, tiled=True)


def y_shift(k):
    return [
        (y * N_CORE + c, (y + k) % N_Y * N_CORE + c) for y in range(N_Y) for c in range(N_CORE)
    ]


def x_shift(k):
    return [(z * N_X + x, z * N_X + (x + k) % N_X) for z in range(N_Z) for x in range(N_X)]


def position():
    m = lax.axis_index("mp").astype(jnp.int32)
    t = lax.axis_index("tensor").astype(jnp.int32)
    return m, lax.rem(t, N_X), lax.rem(t // N_X, 2)


def piece_kernel(x_hbm, out_ref, blocks, arrived):
    m, col, parity = position()
    copies = []
    for d in range(HALF):
        start = pl.multiple_of((((parity * HALF + d) * N_MP + 1 - m) * N_X + col) * 128, 128)
        copies.append(
            pltpu.make_async_copy(x_hbm.at[:, pl.ds(start, 128)], blocks.at[d], arrived.at[d])
        )
    for copy in copies:
        copy.start()
    for d in range(HALF):
        copies[d].wait()
        out_ref[d] = blocks[d].T


def first_kernel(w_hbm, _, out_ref, arrived):
    rows = w_hbm.shape[0] // N_MP
    begin = pl.multiple_of((1 - position()[0]) * rows + CHUNKS[0][0], 32)
    copy = pltpu.make_async_copy(w_hbm.at[pl.ds(begin, out_ref.shape[0])], out_ref, arrived)
    copy.start()
    copy.wait()


def slice_kernel(w_hbm, *refs):
    n = (len(refs) - 1) // 2
    outs, held, sems = refs[:n], refs[n : 2 * n], refs[-1]
    m = position()[0]
    rows = w_hbm.shape[0] // N_MP
    arriving = []
    for k, (begin, size) in enumerate(CHUNKS[1:]):
        begin = pl.multiple_of((1 - m) * rows + begin, 32)
        arriving.append(
            pltpu.make_async_copy(w_hbm.at[pl.ds(begin, size)], held[k], sems.at[k])
        )
    for copy in arriving:
        copy.start()
    leaving = []
    for k in range(n):
        arriving[k].wait()
        leaving.append(pltpu.make_async_copy(held[k], outs[k], sems.at[n + k]))
        leaving[k].start()
    for copy in leaving:
        copy.wait()


def prep_kernel(x_ref, gate_hbm, grad_hbm, own_ref, cot_ref, part_ref, gate_ref, grad_ref, arrived):
    mine, col, _ = position()
    copies = [
        pltpu.make_async_copy(gate_hbm, gate_ref, arrived.at[0]),
        pltpu.make_async_copy(grad_hbm, grad_ref, arrived.at[1]),
    ]
    for copy in copies:
        copy.start()
    inputs = x_ref[...]
    gram_act = lax.dot_general(
        inputs, inputs, (((1,), (1,)), ((), ())), preferred_element_type=jnp.float32
    )
    for d in range(N_DP):
        start = pl.multiple_of(((d * N_MP + mine) * N_X + col) * 128, 128)
        own_ref[d] = x_ref[:, pl.ds(start, 128)].T
    for copy in copies:
        copy.wait()
    gate = gate_ref[...].astype(jnp.float32)
    silu = gate / (1.0 + jnp.exp(-gate))
    cot = (grad_ref[...].astype(jnp.float32) * silu).astype(jnp.bfloat16)
    cot_ref[...] = cot
    gram_cot = lax.dot_general(
        cot, cot, (((1,), (1,)), ((), ())), preferred_element_type=jnp.float32
    )
    part_ref[...] = jnp.full(part_ref.shape, jnp.sum(gram_act * gram_cot), jnp.float32)


def pack_kernel(where, own_ref, kept_ref, swapped_ref, part_ref, out_ref):
    parity = where[2]
    rows = []
    for model in range(N_MP):
        rest = jnp.sum(part_ref[pl.ds(model * N_Z, N_Z), 0, :], axis=0, keepdims=True)
        for _ in range(3):
            short = rest.astype(jnp.bfloat16).astype(jnp.float32)
            rows.append(short)
            rest = rest - short
    rows.append(jnp.zeros((TAIL - len(rows), 128), jnp.float32))
    tail = jnp.concatenate(rows, axis=0).astype(jnp.bfloat16)
    for d in range(N_DP):
        out_ref[d, 0, pl.ds(0, 128), :] = own_ref[d]
        for model in range(2):
            out_ref[d, model, pl.ds(128, TAIL), :] = tail
    for half, ref in ((parity, kept_ref), (1 - parity, swapped_ref)):
        for d in range(HALF):
            out_ref[half * HALF + d, 1, pl.ds(0, 128), :] = ref[d]


def fisher_kernel(n_seq, where, *refs):
    x_refs = refs[:N_X]
    cots = (refs[N_X : N_X + n_seq], refs[N_X + n_seq : N_X + 2 * n_seq])
    w_ref, *weights, lhs, scale = refs[N_X + 2 * n_seq :]
    main, last = weights[:2], weights[2:]
    first = where[N_X + n_seq] == 0
    limit = CLIP_RATIO * math.sqrt(LEN * D * FF)

    @pl.when(pl.program_id(0) == 0)
    def _():
        for piece in range(N_X):
            rows = pl.ds(pl.multiple_of(where[piece] * 128, 128), 128)
            for seq in range(n_seq):
                for model in range(2):
                    lhs[model, seq, rows, :] = x_refs[piece][seq, model, pl.ds(0, 128), :]
        for seq in range(n_seq):
            tails = sum(
                ref[seq, 0, pl.ds(128, TAIL), :].astype(jnp.float32) for ref in x_refs
            )
            squares = [tails[3 * k : 3 * k + 1] + tails[3 * k + 1 : 3 * k + 2] + tails[3 * k + 2 : 3 * k + 3] for k in range(2)]
            for model in range(2):
                square = jnp.where(first, squares[model], squares[1 - model])
                factor = limit / jnp.maximum(jnp.sqrt(square), limit)
                clip = factor * factor
                scale[model, seq] = jnp.broadcast_to(
                    jnp.concatenate([clip] * (scale.shape[3] // 128), axis=1), scale.shape[2:]
                )

    for block in range(4):
        rows = pl.ds(block * 128, 128)
        weighted = []
        for model in range(2):
            total = jnp.full((128, w_ref.shape[1]), FLOOR, jnp.float32)
            for piece in range(n_seq):
                seq = where[N_X + piece]
                grad = jnp.dot(
                    lhs[model, seq, rows, :],
                    cots[model][piece][...],
                    preferred_element_type=jnp.float32,
                )
                total = total + scale[model, seq, pl.ds(0, 1), :] * (grad * grad)
            weighted.append(total)
        inverse = 1.0 / (weighted[0] + weighted[1])
        values = (
            weighted[0] * inverse * w_ref[rows, :].astype(jnp.float32),
            weighted[1] * inverse,
        )
        kept = min(128, main[0].shape[0] - block * 128)
        for value, ref, rest in zip(values, main, last):
            ref[pl.ds(block * 128, kept), :] = value[:kept]
            if kept < 128:
                rest[...] = value[kept:]


def merge_kernel(a_ref, b_ref, w_ref, *refs):
    out_ref = refs[-1]
    out_ref[...] = (a_ref[...] + b_ref[...] * w_ref[...].astype(jnp.float32)).astype(jnp.bfloat16)


def last_merge_kernel(begin, a_ref, b_ref, w_ref, _, out_hbm, done, sem):
    done[...] = (a_ref[...] + b_ref[...] * w_ref[...].astype(jnp.float32)).astype(jnp.bfloat16)
    copy = pltpu.make_async_copy(done, out_hbm.at[pl.ds(begin, done.shape[0])], sem)
    copy.start()
    copy.wait()


def local(activations, gate_pre, hidden_grad, up_weights):
    single = jnp.float32
    width = gate_pre.shape[2]
    m = lax.axis_index("mp").astype(jnp.int32)
    d = lax.axis_index("dp").astype(jnp.int32)
    x = lax.rem(lax.axis_index("tensor").astype(jnp.int32), N_X)
    rows = up_weights.shape[1] // N_MP

    parity = lax.rem(lax.axis_index("tensor").astype(jnp.int32) // N_X, 2)
    place = jnp.stack([m, x, parity])
    piece_shape = jax.ShapeDtypeStruct((N_DP, 128, LEN), jnp.bfloat16)
    half_shape = (HALF, 128, LEN)
    anywhere = pl.BlockSpec(memory_space=pl.ANY)
    first_shape = (CHUNKS[0][1], width)
    other_x = pl.pallas_call(
        piece_kernel,
        out_shape=jax.ShapeDtypeStruct(half_shape, jnp.bfloat16),
        in_specs=[pl.BlockSpec(memory_space=pltpu.HBM)],
        out_specs=pl.BlockSpec(memory_space=pltpu.VMEM),
        scratch_shapes=[
            pltpu.VMEM((HALF, LEN, 128), jnp.bfloat16),
            pltpu.SemaphoreType.DMA((HALF,)),
        ],
        compiler_params=pltpu.CompilerParams(vmem_limit_bytes=PREP_VMEM_LIMIT),
        cost_estimate=pl.CostEstimate(flops=10**5, bytes_accessed=10**6, transcendentals=0),
        name="pieces",
    )(activations[0])
    w_first = pl.pallas_call(
        first_kernel,
        out_shape=jax.ShapeDtypeStruct(first_shape, jnp.bfloat16),
        in_specs=[anywhere, anywhere],
        out_specs=pl.BlockSpec(memory_space=pltpu.VMEM),
        scratch_shapes=[pltpu.SemaphoreType.DMA],
        compiler_params=pltpu.CompilerParams(vmem_limit_bytes=VMEM_LIMIT),
        cost_estimate=pl.CostEstimate(flops=10**5, bytes_accessed=10**6, transcendentals=0),
        name="wfirst",
    )(up_weights[0], other_x)

    vmem = pl.BlockSpec(memory_space=pltpu.VMEM)
    own_x, cot, part = pl.pallas_call(
        prep_kernel,
        out_shape=(
            piece_shape,
            jax.ShapeDtypeStruct((LEN, width), jnp.bfloat16),
            jax.ShapeDtypeStruct((N_Z_ALL, 1, 128), single),
        ),
        in_specs=[
            vmem,
            pl.BlockSpec(memory_space=pltpu.HBM),
            pl.BlockSpec(memory_space=pltpu.HBM),
        ],
        out_specs=[vmem, vmem, vmem],
        scratch_shapes=[
            pltpu.VMEM((LEN, width), jnp.bfloat16),
            pltpu.VMEM((LEN, width), jnp.bfloat16),
            pltpu.SemaphoreType.DMA((2,)),
        ],
        compiler_params=pltpu.CompilerParams(vmem_limit_bytes=VMEM_LIMIT),
        cost_estimate=pl.CostEstimate(flops=4 * 10**8, bytes_accessed=4 * 10**6, transcendentals=0),
        name="prep",
    )(activations[0], gate_pre[0], hidden_grad[0])
    cot_other = lax.ppermute(cot, "mp", MP_SWAP)

    from_other = lax.ppermute(other_x, "mp", MP_SWAP)
    parts = exchange(part, ("mp", "tensor"), Z_GROUPS)
    swapped = lax.ppermute(from_other, "tensor", Z_SWAP)
    packed = pl.pallas_call(
        pack_kernel,
        out_shape=jax.ShapeDtypeStruct((N_DP, 2, 128 + TAIL, LEN), jnp.bfloat16),
        grid_spec=pltpu.PrefetchScalarGridSpec(
            num_scalar_prefetch=1,
            grid=(1,),
            in_specs=[
                pl.BlockSpec((N_DP, 128, LEN), lambda i, w: (0, 0, 0)),
                pl.BlockSpec(half_shape, lambda i, w: (0, 0, 0)),
                pl.BlockSpec(half_shape, lambda i, w: (0, 0, 0)),
                pl.BlockSpec((N_Z_ALL, 1, 128), lambda i, w: (0, 0, 0)),
            ],
            out_specs=pl.BlockSpec((N_DP, 2, 128 + TAIL, LEN), lambda i, w: (0, 0, 0, 0)),
        ),
        compiler_params=pltpu.CompilerParams(vmem_limit_bytes=PREP_VMEM_LIMIT),
        cost_estimate=pl.CostEstimate(flops=10**5, bytes_accessed=10**6, transcendentals=0),
        name="pack",
    )(place, own_x, from_other, swapped, parts)
    x_pieces = exchange(packed, "dp")
    x_all = [x_pieces] + [lax.ppermute(x_pieces, "tensor", x_shift(k)) for k in (1, -1, 2)]
    x_from = [x, lax.rem(x + 3, 4), lax.rem(x + 1, 4), lax.rem(x + 2, 4)]

    later = [(size, width) for _, size in CHUNKS[1:]]
    w_later, _ = lax.optimization_barrier((up_weights[0], part))
    pieces = [w_first] + list(
        pl.pallas_call(
            slice_kernel,
            out_shape=[jax.ShapeDtypeStruct(shape, jnp.bfloat16) for shape in later],
            in_specs=[anywhere],
            out_specs=[anywhere] * len(later),
            scratch_shapes=[pltpu.VMEM(shape, jnp.bfloat16) for shape in later]
            + [pltpu.SemaphoreType.DMA((2 * len(later),))],
            compiler_params=pltpu.CompilerParams(vmem_limit_bytes=PREP_VMEM_LIMIT),
            cost_estimate=pl.CostEstimate(
                flops=10**5, bytes_accessed=3 * 10**6, transcendentals=0
            ),
            name="slices",
        )(w_later)
    )
    w_other = [lax.ppermute(piece, "mp", MP_SWAP) for piece in pieces]

    y = d // N_CORE
    c = lax.rem(d, N_CORE)
    cots, seqs = [], []
    for value in (cot, cot_other):
        pieces = [value] + [lax.ppermute(value, "dp", y_shift(k)) for k in (1, -1, 2)]
        pieces += [lax.ppermute(piece, "dp", CORE_SWAP) for piece in pieces]
        cots += pieces
    for core in (c, 1 - c):
        for shift in (0, 3, 1, 2):
            seqs.append(lax.rem(y + shift, N_Y) * N_CORE + core)

    tile = 256
    n_seq = N_DP
    where = jnp.stack(x_from + seqs).astype(jnp.int32)
    whole = pl.BlockSpec((N_DP, 2, 128 + TAIL, LEN), lambda i, *_: (0, 0, 0, 0))
    last_begin, last_size = CHUNKS[-1]
    a, b, a_last, b_last = pl.pallas_call(
        functools.partial(fisher_kernel, n_seq),
        out_shape=[jax.ShapeDtypeStruct((last_begin, width), single)] * 2
        + [jax.ShapeDtypeStruct((last_size, width), single)] * 2,
        grid_spec=pltpu.PrefetchScalarGridSpec(
            num_scalar_prefetch=1,
            grid=(width // tile,),
            in_specs=[whole] * N_X
            + [pl.BlockSpec((LEN, tile), lambda i, *_: (0, i))] * (2 * n_seq)
            + [pl.BlockSpec((rows, tile), lambda i, w: (w[N_X + n_seq], i))],
            out_specs=[pl.BlockSpec((last_begin, tile), lambda i, *_: (0, i))] * 2
            + [pl.BlockSpec((last_size, tile), lambda i, *_: (0, i))] * 2,
            scratch_shapes=[
                pltpu.VMEM((2, n_seq, rows, LEN), jnp.bfloat16),
                pltpu.VMEM((2, n_seq, 8, tile), single),
            ],
        ),
        compiler_params=pltpu.CompilerParams(vmem_limit_bytes=VMEM_LIMIT),
        cost_estimate=pl.CostEstimate(flops=4 * 10**9, bytes_accessed=18 * 10**6, transcendentals=0),
        name="fisher",
    )(jnp.concatenate([where, m[None]]), *x_all, *cots, up_weights[0])

    out = None
    for k, (begin, chunk) in enumerate(CHUNKS[:-1]):
        half = lambda i, k=begin // chunk: (k, 0)
        first = lambda i: (0, 0)
        in_specs = [pl.BlockSpec((chunk, width), half)] * 2 + [pl.BlockSpec((chunk, width), first)]
        operands = [a, b, w_other[k]]
        aliases = {}
        if out is not None:
            in_specs.append(pl.BlockSpec(memory_space=pl.ANY))
            operands.append(out)
            aliases = {3: 0}
        out = pl.pallas_call(
            merge_kernel,
            out_shape=jax.ShapeDtypeStruct((rows, width), jnp.bfloat16),
            grid=(1,),
            in_specs=in_specs,
            out_specs=pl.BlockSpec((chunk, width), half),
            input_output_aliases=aliases,
            compiler_params=pltpu.CompilerParams(vmem_limit_bytes=PREP_VMEM_LIMIT),
            cost_estimate=pl.CostEstimate(
                flops=chunk * width * 2, bytes_accessed=chunk * width * 12, transcendentals=0
            ),
        )(*operands)
    return pl.pallas_call(
        functools.partial(last_merge_kernel, last_begin),
        out_shape=jax.ShapeDtypeStruct((rows, width), jnp.bfloat16),
        in_specs=[vmem] * 3 + [anywhere],
        out_specs=anywhere,
        scratch_shapes=[
            pltpu.VMEM((last_size, width), jnp.bfloat16),
            pltpu.SemaphoreType.DMA,
        ],
        input_output_aliases={3: 0},
        compiler_params=pltpu.CompilerParams(vmem_limit_bytes=8 * 1024 * 1024),
        cost_estimate=pl.CostEstimate(
            flops=last_size * width * 2, bytes_accessed=last_size * width * 12, transcendentals=0
        ),
        name="merge_last",
    )(a_last, b_last, w_other[-1], out)


def solution(mesh):
    placed = (
        P("mp", "dp", None),
        P("mp", "dp", "tensor"),
        P("mp", "dp", "tensor"),
        P("mp", "dp", "tensor"),
    )

    return jax.shard_map(
        local, mesh=mesh, in_specs=placed, out_specs=P(("dp", "mp"), "tensor"), check_vma=False
    )
```
